32 devices in a mesh: tiles: 2 (over x), morton: 16 (over z, y, core).
Axes of the slice: x: 2, y: 2, z: 4, core: 2. Of those that a mesh axis runs over, the one named last changes fastest.
Arguments:
- features: bfloat16 [256, 512, 64], P(('tiles', 'morton')), parts along dimension 0, may hold values from -6 to 6
- neighbours: int32 [256, 27], P(('tiles', 'morton')), parts along dimension 0, may hold values from -1 to 127, as said below
- occupancy: int32 [256, 16], P(('tiles', 'morton')), parts along dimension 0, may hold values from -2147483648 to 2147483647, as said below
- conv_one: bfloat16 [27, 64, 64], replicated, may hold values from -0.21875 to 0.21875
- first_reduce_kernel: bfloat16 [8, 64, 128], replicated, may hold values from -0.5 to 0.5
- conv_two: bfloat16 [27, 128, 128], replicated, may hold values from -0.1875 to 0.1875
- second_reduce_kernel: bfloat16 [8, 128, 256], replicated, may hold values from -0.375 to 0.375
- conv_three: bfloat16 [27, 256, 256], replicated, may hold values from -0.125 to 0.125
Outputs:
- first_level_features: bfloat16 [256, 512, 64], P(('tiles', 'morton')), parts along dimension 0
- second_level_features: bfloat16 [256, 64, 128], P(('tiles', 'morton')), parts along dimension 0
- skip_three: bfloat16 [256, 8, 256], P(('tiles', 'morton')), parts along dimension 0
The draws below stay inside these ranges and needn't reach their ends.
There are 2 independent parts, one for each index of `tiles`. The reference program is written for one: setup_inputs(seed, part) draws one part's arguments, and reference() takes and returns one part's arrays. A program takes and returns all parts, laid end to end along the dimension named above; an argument that names none is the same for every part. Nothing has to cross between parts.
Inputs may be any that keep to these rules, and one draw needn't show every extreme that they name: `neighbours`: bricks are numbered by x slice, then by cell of the slice's 4 x 4 cross-section in rising order, 8 occupied bricks to a slice. Entry 9 (a+1) + 3 (c+1) + (e+1) of a brick's row is the number of the brick at offset (a, c, e), or -1 if that cell is empty or outside the tile; entry 13 is the brick itself. Every neighbour lies in the brick's own slice or in an adjacent one. Bit k, the lowest being bit 0, of word w of a brick's row is the occupancy of voxel 32 w + k; bit 31 is the sign bit of the word.
All inputs are finite; a program needn't handle non-finite values.
Results may differ from the reference program's by a relative error of at most 0.008.
Values may be sent and summed in bfloat16 or wider, within the bound.
A program may use at most 128 MiB of HBM per device.

```python
import jax
import jax.numpy as jnp
from jax import lax

C1 = 64
C2 = 128
C3 = 256
BRICK_EDGE_VOXELS = 8
SLICE_BRICKS = 8
SLICES = 1
BRICKS = 128
V1 = 512
N_MORTON = 16


def draw_neighbours(key, part):
    slice_total = SLICES * N_MORTON
    scores = jax.random.randint(key, (slice_total, 16), 0, 1 << 20, dtype=jnp.int32) * 16 + jnp.arange(16, dtype=jnp.int32)
    order = jnp.argsort(scores, axis=1)
    ranks = jnp.argsort(order, axis=1)
    filled = (ranks < SLICE_BRICKS).astype(jnp.int32)
    rank_cell = (jnp.cumsum(filled, axis=1) - 1).astype(jnp.int32)
    cells = jnp.argsort(1 - filled, axis=1, stable=True)[:, :SLICE_BRICKS].astype(jnp.int32)
    slice_of = jnp.broadcast_to(jnp.arange(slice_total, dtype=jnp.int32)[:, None], cells.shape)
    row_pos = cells // 4
    col_pos = cells % 4
    entries = []
    for first in (-1, 0, 1):
        for second in (-1, 0, 1):
            for third in (-1, 0, 1):
                near_slice = slice_of + first
                near_row = row_pos + second
                near_col = col_pos + third
                inside = (near_slice >= 0) & (near_slice < slice_total) & (near_row >= 0) & (near_row < 4) & (near_col >= 0) & (near_col < 4)
                safe_slice = jnp.clip(near_slice, 0, slice_total - 1)
                safe_cell = jnp.clip(near_row, 0, 3) * 4 + jnp.clip(near_col, 0, 3)
                present = filled[safe_slice, safe_cell] == 1
                number = safe_slice * SLICE_BRICKS + rank_cell[safe_slice, safe_cell]
                entries.append(jnp.where(inside & present, number, -1).astype(jnp.int32))
    return jnp.stack(entries, axis=-1).reshape(slice_total * SLICE_BRICKS, 27)


def draw_occupancy(key, part):
    brick_side = BRICK_EDGE_VOXELS
    key_list = jax.random.split(key, 6)
    voxel_ids = jnp.arange(brick_side ** 3, dtype=jnp.int32)[None, :]
    depth_index = voxel_ids // (brick_side * brick_side)
    row_index = voxel_ids // brick_side % brick_side
    col_index = voxel_ids % brick_side
    facing = jax.random.randint(key_list[0], (BRICKS, 1), 0, 3, dtype=jnp.int32)
    height_base = jax.random.randint(key_list[1], (BRICKS, 1), 0, brick_side, dtype=jnp.int32)
    tilt_pair = jax.random.randint(key_list[2], (BRICKS, 2), -1, 2, dtype=jnp.int32)
    thickness = jax.random.randint(key_list[3], (BRICKS, 1), brick_side // 4, brick_side // 2 + 2, dtype=jnp.int32)
    present = jax.random.randint(key_list[4], (BRICKS, 1), 0, 8, dtype=jnp.int32) > 0
    retained = jax.random.randint(key_list[5], (BRICKS, brick_side ** 3), 0, 8, dtype=jnp.int32) > 0
    across = jnp.where(facing == 0, depth_index, jnp.where(facing == 1, row_index, col_index))
    along_one = jnp.where(facing == 0, row_index, depth_index)
    along_two = jnp.where(facing == 2, row_index, col_index)
    height = height_base - brick_side // 4 + (tilt_pair[:, 0:1] * along_one + tilt_pair[:, 1:2] * along_two) // 2
    offset = across - height
    occupied = (offset >= 0) & (offset < thickness) & retained & present
    bits = occupied.astype(jnp.int32).reshape(BRICKS, brick_side ** 3 // 32, 32)
    shifted = jnp.left_shift(bits, jnp.arange(32, dtype=jnp.int32))
    return jnp.sum(shifted, axis=-1, dtype=jnp.int32).astype(jnp.int32)


def block_levels(own_key, dims, pieces, least, largest):
    def one(axis_at, blocks):
        heights = jax.random.uniform(jax.random.fold_in(jax.random.fold_in(own_key, 6), axis_at), (blocks,), jnp.float32, least / len(pieces), largest / len(pieces))
        return jnp.repeat(jnp.exp(heights), dims[axis_at] // blocks).reshape((-1,) + (1,) * (len(dims) - axis_at - 1))

    factor_of = one(*pieces[0])
    for cut in pieces[1:]:
        factor_of = factor_of * one(*cut)
    return factor_of


def bell_draw(key, extent, width, bound, pieces=(), held_as=jnp.bfloat16):
    array = width * jax.random.normal(key, extent, jnp.float32)
    if pieces:
        array = array * block_levels(key, extent, pieces, -0.22, 0.18)
    return jnp.clip(array, -bound, bound).astype(held_as)


def setup_inputs(seed: int = 0, part: int = 0) -> dict:
    streams_of = jax.random.split(jax.random.key(seed), 9)
    part_splits = jax.random.split(jax.random.fold_in(streams_of[8], part), 9)
    features = bell_draw(part_splits[0], (BRICKS, V1, C1), 1.0, 6.0, ((0, 16),))
    neighbours = draw_neighbours(jax.random.fold_in(jax.random.fold_in(streams_of[8], part), 71), part)
    occupancy = draw_occupancy(jax.random.fold_in(jax.random.fold_in(streams_of[8], part), 71), part)
    conv_one = bell_draw(streams_of[3], (27, C1, C1), (27 * C1 // 2) ** -0.5, 0.21875)
    first_reduce_kernel = bell_draw(streams_of[4], (8, C1, C2), (2 * C1) ** -0.5, 0.5)
    conv_two = bell_draw(streams_of[5], (27, C2, C2), (9 * C2) ** -0.5, 0.1875)
    second_reduce_kernel = bell_draw(streams_of[6], (8, C2, C3), (2 * C2) ** -0.5, 0.375)
    conv_three = bell_draw(streams_of[7], (27, C3, C3), (9 * C3) ** -0.5, 0.125)
    return {"features": features, "neighbours": neighbours, "occupancy": occupancy, "conv_one": conv_one, "first_reduce_kernel": first_reduce_kernel, "conv_two": conv_two, "second_reduce_kernel": second_reduce_kernel, "conv_three": conv_three}


def unpack_bits(packed, voxel_count):
    shifts = jnp.arange(32, dtype=jnp.int32)
    bits = jnp.bitwise_and(jnp.right_shift(packed[:, :, None], shifts), 1)
    return bits.reshape(packed.shape[0], voxel_count).astype(jnp.float32)


def pool_mask(occupied_voxel_mask, brick_extent):
    count = occupied_voxel_mask.shape[0]
    half = brick_extent // 2
    blocks = occupied_voxel_mask.reshape(count, half, 2, half, 2, half, 2)
    blocks = blocks.transpose(0, 1, 3, 5, 2, 4, 6).reshape(count, half * half * half, 8)
    return jnp.max(blocks, axis=-1)


def reduce_resolution(feature_volume, kernel_weight, occupied_voxel_mask, brick_extent):
    count, voxels, chans = feature_volume.shape
    half = brick_extent // 2
    stacked = feature_volume.reshape(count, half, 2, half, 2, half, 2, chans)
    stacked = stacked.transpose(0, 1, 3, 5, 2, 4, 6, 7).reshape(count * voxels // 8, 8 * chans)
    summed = jnp.dot(stacked, kernel_weight.reshape(8 * chans, kernel_weight.shape[2]), preferred_element_type=jnp.float32)
    result = jnp.maximum(summed, 0.0) * occupied_voxel_mask.reshape(-1, 1)
    return result.astype(jnp.bfloat16).reshape(count, voxels // 8, kernel_weight.shape[2])


def pad_bricks(gathered, brick_extent):
    count, chans = gathered.shape[0], gathered.shape[-1]
    table = ((brick_extent - 1, 1, 0), (0, brick_extent, 1), (0, 1, brick_extent + 1))
    padded = jnp.zeros((count, brick_extent + 2, brick_extent + 2, brick_extent + 2, chans), gathered.dtype)
    for first in range(3):
        for second in range(3):
            for third in range(3):
                tap = first * 9 + second * 3 + third
                src_a, len_a, dst_a = table[first]
                src_b, len_b, dst_b = table[second]
                src_c, len_c, dst_c = table[third]
                piece = gathered[:, tap, src_a:src_a + len_a, src_b:src_b + len_b, src_c:src_c + len_c, :]
                padded = padded.at[:, dst_a:dst_a + len_a, dst_b:dst_b + len_b, dst_c:dst_c + len_c, :].set(piece)
    return padded


def convolve_block(extended, sources, occupied_voxel_mask, kernel_weight, brick_extent):
    count = sources.shape[0]
    chans = extended.shape[-1]
    gathered = extended[sources].reshape(count, 27, brick_extent, brick_extent, brick_extent, chans)
    padded = pad_bricks(gathered, brick_extent)
    windows = []
    for first in range(3):
        for second in range(3):
            for third in range(3):
                windows.append(padded[:, first:first + brick_extent, second:second + brick_extent, third:third + brick_extent, :])
    columns = jnp.concatenate(windows, axis=-1).reshape(count * brick_extent ** 3, 27 * chans)
    summed = jnp.dot(columns, kernel_weight.reshape(27 * chans, kernel_weight.shape[2]), preferred_element_type=jnp.float32)
    result = jnp.maximum(summed, 0.0) * occupied_voxel_mask.reshape(-1, 1)
    return result.astype(jnp.bfloat16).reshape(count, brick_extent ** 3, kernel_weight.shape[2])


def run_level(feature_volume, neighbours, occupied_voxel_mask, kernel_weight, brick_extent):
    total, voxels, chans = feature_volume.shape
    extended = jnp.concatenate([feature_volume, jnp.zeros((1, voxels, chans), feature_volume.dtype)], axis=0)
    sources = jnp.where(neighbours < 0, total, neighbours).astype(jnp.int32)
    groups = total // SLICE_BRICKS

    def one_block(pair):
        return convolve_block(extended, pair[0], pair[1], kernel_weight, brick_extent)

    blocks = (sources.reshape(groups, SLICE_BRICKS, 27), occupied_voxel_mask.reshape(groups, SLICE_BRICKS, voxels))
    return lax.map(one_block, blocks).reshape(total, voxels, kernel_weight.shape[2])


def reference(features, neighbours, occupancy, conv_one, first_reduce_kernel, conv_two, second_reduce_kernel, conv_three):
    mask_one = unpack_bits(occupancy, BRICK_EDGE_VOXELS ** 3)
    second_level_mask = pool_mask(mask_one, BRICK_EDGE_VOXELS)
    third_level_mask = pool_mask(second_level_mask, BRICK_EDGE_VOXELS // 2)
    input_one = (features.astype(jnp.float32) * mask_one[:, :, None]).astype(jnp.bfloat16)
    first_level_features = run_level(input_one, neighbours, mask_one, conv_one, BRICK_EDGE_VOXELS)
    second_level_input = reduce_resolution(first_level_features, first_reduce_kernel, second_level_mask, BRICK_EDGE_VOXELS)
    second_level_features = run_level(second_level_input, neighbours, second_level_mask, conv_two, BRICK_EDGE_VOXELS // 2)
    third_level_input = reduce_resolution(second_level_features, second_reduce_kernel, third_level_mask, BRICK_EDGE_VOXELS // 2)
    skip_three = run_level(third_level_input, neighbours, third_level_mask, conv_three, BRICK_EDGE_VOXELS // 4)
    return first_level_features, second_level_features, skip_three
```

```python
import jax
import jax.numpy as jnp
from jax import lax
from jax.experimental import pallas as pl
from jax.experimental.pallas import tpu as pltpu
from jax.sharding import PartitionSpec as P

BRICKS = 8
F32 = jnp.float32
BF16 = jnp.bfloat16
I32 = jnp.int32


def iota(shape, dim):
    return lax.broadcasted_iota(I32, shape, dim)


def pack(lower, upper):
    return jnp.concatenate([lower, upper], axis=0).astype(BF16)


def halves(tile):
    wide = tile.astype(F32)
    return wide[0:8], wide[8:16]


def windows_one(own, before, after):
    low_lanes = iota((BRICKS, 128), 1) < 64
    return (
        (own[0], own[2]),
        (own[1], own[3]),
        (jnp.where(low_lanes, own[2], before(3)), jnp.where(low_lanes, after(0), own[1])),
    )


def windows_two(own, before, after):
    return ((own[0], own[2]), (own[1], own[3]), (own[2], after(0)), (before(3), own[1]))


def windows_three(own, before, after):
    return (
        (before(2), own[0]), (before(3), own[1]),
        (own[0], own[2]), (own[1], own[3]),
        (own[2], after(0)), (own[3], after(1)),
    )


def fill(put, tiles, dx, dy, near, windows):
    first = 9 * dx + 3 * dy

    def moved(q, tap):
        number = near[tap]
        picked = jnp.take_along_axis(tiles[q], number & (BRICKS - 1), axis=0, mode="promise_in_bounds")
        return jnp.where(number >= 0, picked, 0.0)

    own = tiles if first == 12 else [moved(q, first + 1) for q in range(4)]
    for at, (lower, upper) in enumerate(
        windows(own, lambda q: moved(q, first), lambda q: moved(q, first + 2))
    ):
        put(at, pack(lower, upper))


def fill_plane(side, cols, to, source, dx, near, windows):
    for j in range(side):
        tiles = source(j)
        places = [(1, j + 1)] + [(0, 0)] * (j == side - 1) + [(2, side + 1)] * (j == 0)
        for dy, column in places:
            def put(at, value, column=column):
                cols[to, column, :, 128 * at : 128 * at + 128] = value
            fill(put, tiles, dx, dy, near, windows)


def convolve(side, planes, cols, band):
    width = cols.shape[-1]
    left = jnp.concatenate(
        [
            jnp.concatenate(
                [cols[plane + a, c : c + side].reshape(side * 16, width) for plane in planes], axis=0
            )
            for a in range(3)
            for c in range(3)
        ],
        axis=1,
    )
    return jnp.dot(left, band, preferred_element_type=F32)


def build_band_one(source, band):
    @pl.loop(0, 9)
    def _(pair):
        minus, same, plus = (source[3 * pair + e] for e in range(3))
        zero = jnp.zeros_like(same)
        blank = jnp.zeros((64, 128), BF16)
        low = jnp.concatenate([same, minus], axis=1)
        high = jnp.concatenate([plus, same], axis=1)
        before = jnp.concatenate([minus, zero], axis=1)
        after = jnp.concatenate([zero, plus], axis=1)
        rows = ((low, blank), (high, before), (after, low), (blank, high), (blank, after), (before, blank))
        for at, (left, right) in enumerate(rows):
            to = pl.ds(pl.multiple_of(384 * pair + 64 * at, 64), 64)
            band[to, 0:128] = left
            band[to, 128:256] = right


def build_band_two(source, band):
    @pl.loop(0, 9)
    def _(pair):
        minus, same, plus = (source[3 * pair + e] for e in range(3))
        blank = jnp.zeros_like(same)
        rows = ((same, minus), (plus, same), (blank, plus), (minus, blank))
        for at, (left, right) in enumerate(rows):
            to = pl.ds(pl.multiple_of(512 * pair + 128 * at, 128), 128)
            band[to, 0:128] = left
            band[to, 128:256] = right


def fused(nb, feat, occ, conv_one, kernel_one, conv_two_hbm, kernel_two_hbm, conv_three_hbm,
          out_one, out_two, cols_three, pooled_three, conv_three,
          field_one, field_two, field_three, cols_one, cols_two, done_one, done_two,
          band_one, band_two, conv_two, kernel_two, near, words, tests, pooled_two, wide,
          outgoing, incoming, load_sems, send_sems, recv_sems):
    me = lax.axis_index("morton")
    count = lax.axis_size("morton")
    has_low, has_high = me > 0, me < count - 1
    sides = ((has_low, me - 1), (has_high, me + 1))
    extents = (8, 4, 2)

    loads = [
        pltpu.make_async_copy(source, target, load_sems.at[at])
        for at, (source, target) in enumerate(
            ((conv_two_hbm, conv_two), (kernel_two_hbm, kernel_two), (conv_three_hbm, conv_three))
        )
    ]
    for load in loads:
        load.start()

    barrier = pltpu.get_barrier_semaphore()
    for there, device in sides:
        @pl.when(there)
        def _():
            pl.semaphore_signal(barrier, inc=1, device_id={"morton": device},
                                device_id_type=pl.DeviceIdType.MESH)

    def transfer(level, to):
        return pltpu.make_async_remote_copy(
            src_ref=outgoing.at[level, to, 0 : extents[level]],
            dst_ref=incoming.at[level, 1 - to, 0 : extents[level]],
            send_sem=send_sems.at[level, to],
            recv_sem=recv_sems.at[level, 1 - to],
            device_id={"morton": sides[to][1]},
            device_id_type=pl.DeviceIdType.MESH,
        )

    def send(level):
        for to in range(2):
            @pl.when(sides[to][0])
            def _():
                transfer(level, to).start()

    def receive(level, cols, windows):
        side = extents[level]
        for source in range(2):
            @pl.when(sides[source][0])
            def _():
                transfer(level, 1 - source).wait_recv()

            def arrived(j, source=source):
                pieces = [halves(incoming[level, source, j, :, 128 * t : 128 * t + 128]) for t in range(2)]
                return [pieces[q % 2][q // 2] for q in range(4)]

            fill_plane(side, cols, (0, side + 1)[source], arrived, 2 * source, near, windows)

    def stage(level, to, j, tiles):
        for t in range(2):
            outgoing[level, to, j, :, 128 * t : 128 * t + 128] = pack(tiles[t], tiles[2 + t])

    for source in range(2):
        @pl.when(jnp.logical_not(sides[source][0]))
        def _():
            for level in range(3):
                incoming[level, source] = jnp.zeros(incoming.shape[2:], BF16)

    for tap in range(27):
        near[tap] = jnp.broadcast_to(nb[:, tap : tap + 1], (BRICKS, 128))
    for word in range(16):
        words[word] = jnp.broadcast_to(occ[:, word : word + 1], (BRICKS, 128))
    upper = (iota((BRICKS, 128), 1) >= 64).astype(I32)
    for at in range(16):
        tests[at] = jnp.left_shift(jnp.ones((BRICKS, 128), I32), 2 * at + upper)
    for i in range(4):
        for part in range(2):
            word = words[4 * i + part] | words[4 * i + 2 + part]
            for far in range(2):
                pooled_two[i, 2 * part + far] = (word >> (16 * far)) | (word >> (16 * far + 8))
    for i in range(2):
        for j in range(2):
            pooled_three[i, j] = (
                pooled_two[2 * i, 2 * j] | pooled_two[2 * i, 2 * j + 1]
                | pooled_two[2 * i + 1, 2 * j] | pooled_two[2 * i + 1, 2 * j + 1]
            )

    def keep_one(i, j, q, value):
        bit = words[2 * i + j // 4] & tests[4 * (j % 4) + q]
        return jnp.where(bit != 0, value, 0.0)

    choose = (iota((128, 256), 1) // 2 == iota((128, 256), 0)).astype(F32).astype(BF16)
    odd = iota((64, 256), 1) % 2 == 1
    for half in range(2):
        lanes = slice(256 * half, 256 * half + 256)
        for b in range(0, BRICKS, 2):
            rows = []
            for brick in (b, b + 1):
                value = feat[brick, :, lanes]
                zero = jnp.zeros_like(value)
                rows += [jnp.where(odd, zero, value), jnp.where(odd, value, zero)]
            both = lax.dot_general(
                choose, jnp.concatenate(rows, axis=0), (((1,), (1,)), ((), ())),
                preferred_element_type=F32,
            )
            for step in range(2):
                field_one[pl.ds(1024 * half + b + step, 128, stride=8), :] = (
                    both[:, 128 * step : 128 * step + 128]
                )

    def tile_at(i, j, q):
        return pl.ds(pl.multiple_of(256 * i + 32 * j + 8 * q, 8), 8)

    def own_one(i):
        def source(j):
            return [keep_one(i, j, q, field_one[tile_at(i, j, q), :]) for q in range(4)]
        return source

    for to, i in enumerate((0, 7)):
        def edge(j, to=to, i=i):
            tiles = own_one(i)(j)
            stage(0, to, j, tiles)
            return tiles
        fill_plane(8, cols_one, i + 1, edge, 1, near, windows_one)

    pl.semaphore_wait(barrier, jnp.minimum(me, 1) + jnp.minimum(count - 1 - me, 1))
    send(0)
    build_band_one(conv_one, band_one)

    @pl.loop(1, 7)
    def _(i):
        fill_plane(8, cols_one, i + 1, own_one(i), 1, near, windows_one)

    loads[0].wait()
    build_band_two(conv_two, band_two)
    receive(0, cols_one, windows_one)

    def first_level(planes):
        sums = convolve(8, planes, cols_one, band_one[...])
        for p, i in enumerate(planes):
            for j in range(8):
                at = 128 * p + 16 * j
                for t in range(2):
                    lanes = slice(128 * t, 128 * t + 128)
                    tiles = []
                    for h in range(2):
                        q = 2 * h + t
                        value = keep_one(i, j, q, jnp.maximum(sums[at + 8 * h : at + 8 * h + 8, lanes], 0.0))
                        field_one[tile_at(i, j, q), :] = value
                        tiles.append(value)
                    done_one[i, j, :, lanes] = pack(*tiles)
        pooled = [planes[0] // 2, planes[2] // 2]
        left = jnp.concatenate(
            [
                jnp.concatenate(
                    [
                        done_one[2 * i + ci, 2 * j + cj, :, 128 * t : 128 * t + 128]
                        for t in range(2)
                        for i in pooled
                        for j in range(4)
                    ],
                    axis=0,
                )
                for ci in range(2)
                for cj in range(2)
            ],
            axis=1,
        )
        sums = jnp.dot(left, kernel_one[...], preferred_element_type=F32)
        for p, i in enumerate(pooled):
            for j in range(4):
                for t in range(2):
                    for h in range(2):
                        at = 128 * t + 64 * p + 16 * j + 8 * h
                        q = 2 * h + t
                        keep = (pooled_two[i, j] & (3 << (2 * q))) != 0
                        field_two[i, j, q] = jnp.where(keep, jnp.maximum(sums[at : at + 8], 0.0), 0.0)

    first_level((0, 1, 6, 7))
    for to, i in enumerate((0, 3)):
        for j in range(4):
            stage(1, to, j, [field_two[i, j, q] for q in range(4)])
    send(1)
    first_level((2, 3, 4, 5))

    for i in range(4):
        fill_plane(4, cols_two, i + 1, lambda j, i=i: [field_two[i, j, q] for q in range(4)],
                   1, near, windows_two)
    receive(1, cols_two, windows_two)

    sums = convolve(4, range(4), cols_two, band_two[...])
    for i in range(4):
        for j in range(4):
            at = 64 * i + 16 * j
            for t in range(2):
                lanes = slice(128 * t, 128 * t + 128)
                tiles = []
                for h in range(2):
                    q = 2 * h + t
                    keep = (pooled_two[i, j] & (3 << (2 * q))) != 0
                    value = jnp.where(keep, jnp.maximum(sums[at + 8 * h : at + 8 * h + 8, lanes], 0.0), 0.0)
                    wide[pl.ds(16 * i + 4 * j + q, 8, stride=64), :] = value
                    tiles.append(value)
                done_two[i, j, :, lanes] = pack(*tiles)
    loads[1].wait()
    left = jnp.concatenate(
        [
            jnp.concatenate(
                [done_two[2 * i + ci, 2 * j + cj] for i in range(2) for j in range(2)], axis=0
            )
            for ci in range(2)
            for cj in range(2)
        ],
        axis=1,
    )
    sums = jnp.dot(left, kernel_two[...], preferred_element_type=F32)
    for i in range(2):
        for j in range(2):
            at = 32 * i + 16 * j
            for h in range(2):
                keep = (pooled_three[i, j] & (15 << (4 * h))) != 0
                for t in range(2):
                    value = sums[at + 8 * h : at + 8 * h + 8, 128 * t : 128 * t + 128]
                    field_three[i, j, 2 * h + t] = jnp.where(keep, jnp.maximum(value, 0.0), 0.0)
    for to in range(2):
        for j in range(2):
            stage(2, to, j, [field_three[to, j, q] for q in range(4)])
    send(2)

    for i in range(2):
        fill_plane(2, cols_three, i + 1, lambda j, i=i: [field_three[i, j, q] for q in range(4)],
                   1, near, windows_three)
    out_two[...] = wide[...].reshape(BRICKS, 64, 128).astype(BF16)

    spread = (
        iota((256, 256), 1) == 2 * (iota((256, 256), 0) % 128) + iota((256, 256), 0) // 128
    ).astype(F32).astype(BF16)
    for half in range(2):
        left = []
        for b in range(BRICKS):
            turned = field_one[pl.ds(1024 * half + b, 128, stride=8), :].T
            left.append(jnp.concatenate([turned[0:64], turned[64:128]], axis=1).astype(BF16))
        sums = jnp.dot(jnp.concatenate(left, axis=0), spread, preferred_element_type=F32)
        for b in range(BRICKS):
            out_one[b, :, 256 * half : 256 * half + 256] = sums[64 * b : 64 * b + 64].astype(BF16)

    receive(2, cols_three, windows_three)

    loads[2].wait()
    for level in range(3):
        for to in range(2):
            @pl.when(sides[to][0])
            def _():
                transfer(level, to).wait_send()


def last_level(one, two, cols_three, pooled_three, conv_three,
               out_one, out_two, out_three, wide, sems):
    copies = [
        pltpu.make_async_copy(one, out_one, sems.at[0]),
        pltpu.make_async_copy(two, out_two, sems.at[1]),
    ]
    for copy in copies:
        copy.start()
    sums = convolve(2, range(2), cols_three, conv_three[...].reshape(27 * 256, 256))
    for i in range(2):
        for j in range(2):
            at = 32 * i + 16 * j
            for h in range(2):
                keep = (pooled_three[i, j] & (15 << (4 * h))) != 0
                for t in range(2):
                    value = sums[at + 8 * h : at + 8 * h + 8, 128 * t : 128 * t + 128]
                    wide[t, pl.ds(4 * i + 2 * j + h, 8, stride=8), :] = jnp.where(
                        keep, jnp.maximum(value, 0.0), 0.0
                    )
    for t in range(2):
        out_three[:, :, 128 * t : 128 * t + 128] = wide[t].reshape(BRICKS, 8, 128).astype(BF16)
    for copy in copies:
        copy.wait()


def on_device(features, neighbours, occupancy, conv_one, first_reduce_kernel,
              conv_two, second_reduce_kernel, conv_three):
    vm = pl.BlockSpec(memory_space=pltpu.VMEM)
    hbm = pl.BlockSpec(memory_space=pltpu.HBM)
    kernel_two = second_reduce_kernel.reshape(1024, 256)
    scratch = [
        ((2048, 128), F32), ((4, 4, 4, BRICKS, 128), F32), ((2, 2, 4, BRICKS, 128), F32),
        ((10, 10, 16, 384), BF16), ((6, 6, 16, 512), BF16),
        ((8, 8, 16, 256), BF16), ((4, 4, 16, 256), BF16),
        ((9 * 384, 256), BF16), ((9 * 512, 256), BF16),
        (conv_two.shape, BF16), (kernel_two.shape, BF16),
        ((27, BRICKS, 128), I32), ((16, BRICKS, 128), I32), ((16, BRICKS, 128), I32),
        ((4, 4, BRICKS, 128), I32), ((512, 128), F32),
        ((3, 2, 8, 16, 256), BF16), ((3, 2, 8, 16, 256), BF16),
    ]
    shapes = [
        jax.ShapeDtypeStruct((BRICKS, 64, 512), BF16),
        jax.ShapeDtypeStruct((BRICKS, 64, 128), BF16),
    ]
    first, second, cols, pooled, weights = pl.pallas_call(
        fused,
        out_shape=shapes
        + [
            jax.ShapeDtypeStruct((4, 4, 16, 768), BF16),
            jax.ShapeDtypeStruct((2, 2, BRICKS, 128), I32),
            jax.ShapeDtypeStruct(conv_three.shape, BF16),
        ],
        in_specs=[vm, vm, vm, vm, vm, hbm, hbm, hbm],
        out_specs=[vm] * 5,
        scratch_shapes=[pltpu.VMEM(shape, dtype) for shape, dtype in scratch]
        + [pltpu.SemaphoreType.DMA((3,)), pltpu.SemaphoreType.DMA((3, 2)),
           pltpu.SemaphoreType.DMA((3, 2))],
        compiler_params=pltpu.CompilerParams(
            collective_id=0, has_side_effects=True, vmem_limit_bytes=36 << 20
        ),
    )(*(
        pltpu.with_memory_space_constraint(x, pltpu.HBM)
        for x in (neighbours, jnp.swapaxes(features, 1, 2), occupancy, conv_one,
                  first_reduce_kernel.reshape(512, 128), conv_two, kernel_two, conv_three)
    ))
    first, second, third = pl.pallas_call(
        last_level,
        out_shape=shapes + [jax.ShapeDtypeStruct((BRICKS, 8, 256), BF16)],
        in_specs=[vm] * 5,
        out_specs=[hbm, hbm, vm],
        scratch_shapes=[pltpu.VMEM((2, 64, 128), F32), pltpu.SemaphoreType.DMA((2,))],
        compiler_params=pltpu.CompilerParams(vmem_limit_bytes=16 << 20),
    )(first, second, cols, pooled, weights)
    return jnp.swapaxes(first, 1, 2), second, third


def solution(mesh):
    split = P(("tiles", "morton"), None, None)
    flat = P(("tiles", "morton"), None)
    return jax.shard_map(
        on_device,
        mesh=mesh,
        in_specs=(split, flat, flat, P(), P(), P(), P(), P()),
        out_specs=(split, split, split),
        check_vma=False,
    )
```

```python
import jax
import jax.numpy as jnp
from jax import lax
from jax.experimental import pallas as pl
from jax.experimental.pallas import tpu as pltpu
from jax.sharding import PartitionSpec as P

BRICKS = 8
F32 = jnp.float32
BF16 = jnp.bfloat16
I32 = jnp.int32


def iota(shape, dim):
    return lax.broadcasted_iota(I32, shape, dim)


def pack(lower, upper):
    return jnp.concatenate([lower, upper], axis=0).astype(BF16)


def halves(tile):
    wide = tile.astype(F32)
    return wide[0:8], wide[8:16]


def windows_one(own, before, after):
    low_lanes = iota((BRICKS, 128), 1) < 64
    return (
        (own[0], own[2]),
        (own[1], own[3]),
        (jnp.where(low_lanes, own[2], before(3)), jnp.where(low_lanes, after(0), own[1])),
    )


def windows_two(own, before, after):
    return ((before(3), own[1]), (own[0], own[2]), (own[1], own[3]), (own[2], after(0)))


def windows_three(own, before, after):
    return (
        (before(2), own[0]), (before(3), own[1]),
        (own[0], own[2]), (own[1], own[3]),
        (own[2], after(0)), (own[3], after(1)),
    )


def fill(put, tiles, dx, dy, near, windows):
    first = 9 * dx + 3 * dy

    def moved(q, tap):
        number = near[tap]
        picked = jnp.take_along_axis(tiles[q], number & (BRICKS - 1), axis=0, mode="promise_in_bounds")
        return jnp.where(number >= 0, picked, 0.0)

    own = tiles if first == 12 else [moved(q, first + 1) for q in range(4)]
    for at, (lower, upper) in enumerate(
        windows(own, lambda q: moved(q, first), lambda q: moved(q, first + 2))
    ):
        put(at, pack(lower, upper))


def fill_plane(side, cols, to, source, dx, near, windows):
    for j in range(side):
        tiles = source(j)
        places = [(1, j + 1)] + [(0, 0)] * (j == side - 1) + [(2, side + 1)] * (j == 0)
        for dy, column in places:
            def put(at, value, column=column):
                cols[to, column, :, 128 * at : 128 * at + 128] = value
            fill(put, tiles, dx, dy, near, windows)


def columns(side, cols, planes, rows_of_taps, lanes, with_halo):
    def block(plane, c):
        if not with_halo and plane in (0, side + 1):
            return jnp.zeros((side * 16, lanes[0].stop - lanes[0].start), BF16)
        return [cols[plane, c : c + side, :, at].reshape(side * 16, at.stop - at.start) for at in lanes]

    def rows(a, c):
        blocks = [block(plane + a, c) for plane in planes]
        return jnp.concatenate(
            [part if not isinstance(part, list) else part[t] for t in range(len(lanes)) for part in blocks],
            axis=0,
        )

    return jnp.concatenate([rows(a, c) for a in rows_of_taps for c in range(3)], axis=1)


def build_band_one(source, band):
    @pl.loop(0, 9)
    def _(pair):
        minus, same, plus = (source[3 * pair + e] for e in range(3))
        zero = jnp.zeros_like(same)
        blank = jnp.zeros((64, 128), BF16)
        low = jnp.concatenate([same, minus], axis=1)
        high = jnp.concatenate([plus, same], axis=1)
        before = jnp.concatenate([minus, zero], axis=1)
        after = jnp.concatenate([zero, plus], axis=1)
        rows = ((low, blank), (high, before), (after, low), (blank, high), (blank, after), (before, blank))
        for at, (left, right) in enumerate(rows):
            to = pl.ds(pl.multiple_of(384 * pair + 64 * at, 64), 64)
            band[to, 0:128] = left
            band[to, 128:256] = right


WIDE_ONE = (slice(0, 384),)
WIDE_TWO = (slice(0, 384), slice(128, 512))
WIDE_THREE = (slice(0, 768),)


def dot(left, right):
    return jnp.dot(left, right, preferred_element_type=F32)


def halo_sums(side, cols, lanes, weights):
    for plane, a in ((0, 0), (side - 1, 2)):
        left = columns(side, cols, (plane,), (a,), lanes, True)
        depth = left.shape[1]
        yield plane, dot(left, weights(a, depth))


def fused(nb_hbm, feat_hbm, occ_hbm, conv_one_hbm, kernel_one_hbm,
          conv_two_hbm, kernel_two_hbm, conv_three_hbm,
          out_one, out_two, cols_three, pooled_three, early_three, conv_three,
          nb, feat, occ, conv_one, kernel_one, conv_two, kernel_two,
          field_one, field_two, field_three, cols_one, cols_two, done_one, done_two,
          band_one, early_one, early_two, near, words, tests, pooled_two, wide,
          choose, spread, regroup, outgoing, incoming, load_sems, send_sems, recv_sems):
    me = lax.axis_index("morton")
    count = lax.axis_size("morton")
    has_low, has_high = me > 0, me < count - 1
    sides = ((has_low, me - 1), (has_high, me + 1))
    extents = (8, 4, 2)

    loads = [
        pltpu.make_async_copy(source, target, load_sems.at[at])
        for at, (source, target) in enumerate(
            (
                (nb_hbm, nb), (occ_hbm, occ), (feat_hbm, feat), (conv_one_hbm, conv_one),
                (kernel_one_hbm, kernel_one), (conv_two_hbm, conv_two),
                (kernel_two_hbm, kernel_two), (conv_three_hbm, conv_three),
            )
        )
    ]
    for load in loads:
        load.start()

    barrier = pltpu.get_barrier_semaphore()
    for there, device in sides:
        @pl.when(there)
        def _():
            pl.semaphore_signal(barrier, inc=1, device_id={"morton": device},
                                device_id_type=pl.DeviceIdType.MESH)

    def transfer(level, to):
        return pltpu.make_async_remote_copy(
            src_ref=outgoing.at[level, to, 0 : extents[level]],
            dst_ref=incoming.at[level, 1 - to, 0 : extents[level]],
            send_sem=send_sems.at[level, to],
            recv_sem=recv_sems.at[level, 1 - to],
            device_id={"morton": sides[to][1]},
            device_id_type=pl.DeviceIdType.MESH,
        )

    def send(level):
        for to in range(2):
            @pl.when(sides[to][0])
            def _():
                transfer(level, to).start()

    def receive(level, cols, windows):
        side = extents[level]
        for source in range(2):
            @pl.when(sides[source][0])
            def _():
                transfer(level, 1 - source).wait_recv()

            def arrived(j, source=source):
                pieces = [halves(incoming[level, source, j, :, 128 * t : 128 * t + 128]) for t in range(2)]
                return [pieces[q % 2][q // 2] for q in range(4)]

            fill_plane(side, cols, (0, side + 1)[source], arrived, 2 * source, near, windows)

    def stage(level, to, j, tiles):
        for t in range(2):
            outgoing[level, to, j, :, 128 * t : 128 * t + 128] = pack(tiles[t], tiles[2 + t])

    for source in range(2):
        @pl.when(jnp.logical_not(sides[source][0]))
        def _():
            for level in range(3):
                incoming[level, source] = jnp.zeros(incoming.shape[2:], BF16)

    row, lane = iota((256, 256), 0), iota((256, 256), 1)
    spread[...] = (lane == 2 * (row % 128) + row // 128).astype(F32).astype(BF16)
    regroup[...] = ((lane // 8 == row % 32) & (lane % 8 == row // 32)).astype(F32).astype(BF16)
    choose[...] = (iota((128, 256), 1) // 2 == iota((128, 256), 0)).astype(F32).astype(BF16)
    upper = (iota((BRICKS, 128), 1) >= 64).astype(I32)
    for at in range(16):
        tests[at] = jnp.left_shift(jnp.ones((BRICKS, 128), I32), 2 * at + upper)

    loads[0].wait()
    loads[1].wait()
    for tap in range(27):
        near[tap] = jnp.broadcast_to(nb[:, tap : tap + 1], (BRICKS, 128))
    for word in range(16):
        words[word] = jnp.broadcast_to(occ[:, word : word + 1], (BRICKS, 128))
    for i in range(4):
        for part in range(2):
            word = words[4 * i + part] | words[4 * i + 2 + part]
            for far in range(2):
                pooled_two[i, 2 * part + far] = (word >> (16 * far)) | (word >> (16 * far + 8))
    for i in range(2):
        for j in range(2):
            pooled_three[i, j] = (
                pooled_two[2 * i, 2 * j] | pooled_two[2 * i, 2 * j + 1]
                | pooled_two[2 * i + 1, 2 * j] | pooled_two[2 * i + 1, 2 * j + 1]
            )

    def keep_one(i, j, q, value):
        bit = words[2 * i + j // 4] & tests[4 * (j % 4) + q]
        return jnp.where(bit != 0, value, 0.0)

    loads[2].wait()
    odd = iota((64, 256), 1) % 2 == 1
    for half in range(2):
        lanes = slice(256 * half, 256 * half + 256)
        for b in range(0, BRICKS, 2):
            rows = []
            for brick in (b, b + 1):
                value = feat[brick, :, lanes]
                zero = jnp.zeros_like(value)
                rows += [jnp.where(odd, zero, value), jnp.where(odd, value, zero)]
            both = lax.dot_general(
                choose[...], jnp.concatenate(rows, axis=0), (((1,), (1,)), ((), ())),
                preferred_element_type=F32,
            )
            for step in range(2):
                field_one[pl.ds(1024 * half + b + step, 128, stride=8), :] = (
                    both[:, 128 * step : 128 * step + 128]
                )

    def tile_at(i, j, q):
        return pl.ds(pl.multiple_of(256 * i + 32 * j + 8 * q, 8), 8)

    def own_one(i):
        def source(j):
            return [keep_one(i, j, q, field_one[tile_at(i, j, q), :]) for q in range(4)]
        return source

    for to, i in enumerate((0, 7)):
        def edge(j, to=to, i=i):
            tiles = own_one(i)(j)
            stage(0, to, j, tiles)
            return tiles
        fill_plane(8, cols_one, i + 1, edge, 1, near, windows_one)

    pl.semaphore_wait(barrier, jnp.minimum(me, 1) + jnp.minimum(count - 1 - me, 1))
    send(0)
    loads[3].wait()
    build_band_one(conv_one, band_one)

    @pl.loop(1, 7)
    def _(i):
        fill_plane(8, cols_one, i + 1, own_one(i), 1, near, windows_one)

    def finish_one(i, sums):
        for j in range(8):
            for t in range(2):
                lanes = slice(128 * t, 128 * t + 128)
                tiles = []
                for h in range(2):
                    q = 2 * h + t
                    at = 16 * j + 8 * h
                    value = keep_one(i, j, q, jnp.maximum(sums[at : at + 8, lanes], 0.0))
                    field_one[tile_at(i, j, q), :] = value
                    tiles.append(value)
                done_one[i, j, :, lanes] = pack(*tiles)

    def reduce_one(pooled):
        left = jnp.concatenate(
            [
                jnp.concatenate(
                    [
                        done_one[2 * i + ci, 2 * j + cj, :, 128 * t : 128 * t + 128]
                        for t in range(2)
                        for i in pooled
                        for j in range(4)
                    ],
                    axis=0,
                )
                for ci in range(2)
                for cj in range(2)
            ],
            axis=1,
        )
        sums = dot(left, kernel_one[...])
        for p, i in enumerate(pooled):
            for j in range(4):
                for t in range(2):
                    for h in range(2):
                        at = 128 * t + 64 * p + 16 * j + 8 * h
                        q = 2 * h + t
                        keep = (pooled_two[i, j] & (3 << (2 * q))) != 0
                        field_two[i, j, q] = jnp.where(keep, jnp.maximum(sums[at : at + 8], 0.0), 0.0)

    def own_two(i):
        return lambda j: [field_two[i, j, q] for q in range(4)]

    sums = dot(columns(8, cols_one, range(8), range(3), WIDE_ONE, False), band_one[...])
    for i in range(8):
        part = sums[128 * i : 128 * i + 128]
        if i in (0, 7):
            early_one[i // 7] = part
        else:
            finish_one(i, part)
    loads[4].wait()
    reduce_one((1, 2))
    receive(0, cols_one, windows_one)
    for i, sums in halo_sums(8, cols_one, WIDE_ONE, lambda a, depth: band_one[a * depth : (a + 1) * depth]):
        finish_one(i, early_one[i // 7] + sums)
    reduce_one((0, 3))
    for to, i in enumerate((0, 3)):
        for j in range(4):
            stage(1, to, j, own_two(i)(j))
    send(1)

    def finish_two(i, sums):
        for j in range(4):
            for t in range(2):
                tiles = []
                for h in range(2):
                    q = 2 * h + t
                    at = 64 * t + 16 * j + 8 * h
                    keep = (pooled_two[i, j] & (3 << (2 * q))) != 0
                    tiles.append(jnp.where(keep, jnp.maximum(sums[at : at + 8], 0.0), 0.0))
                done_two[i, j, :, 128 * t : 128 * t + 128] = pack(*tiles)

    for i in range(4):
        fill_plane(4, cols_two, i + 1, own_two(i), 1, near, windows_two)
    loads[5].wait()
    sums = dot(
        columns(4, cols_two, range(4), range(3), WIDE_TWO, False),
        conv_two[...].reshape(27 * 128, 128),
    )
    for i in range(4):
        part = jnp.concatenate([sums[256 * t + 64 * i : 256 * t + 64 * i + 64] for t in range(2)], axis=0)
        if i in (0, 3):
            early_two[i // 3] = part
        else:
            finish_two(i, part)

    for half in range(2):
        left = []
        for b in range(BRICKS):
            turned = field_one[pl.ds(1024 * half + b, 128, stride=8), :].astype(BF16).T
            left.append(jnp.concatenate([turned[0:64], turned[64:128]], axis=1))
        sums = dot(jnp.concatenate(left, axis=0), spread[...])
        for b in range(BRICKS):
            out_one[b, :, 256 * half : 256 * half + 256] = sums[64 * b : 64 * b + 64].astype(BF16)

    receive(1, cols_two, windows_two)
    for i, sums in halo_sums(
        4, cols_two, WIDE_TWO, lambda a, depth: conv_two[9 * a : 9 * a + 9].reshape(depth, 128)
    ):
        finish_two(i, early_two[i // 3] + sums)
    loads[6].wait()
    left = jnp.concatenate(
        [
            jnp.concatenate(
                [done_two[2 * i + ci, 2 * j + cj] for i in range(2) for j in range(2)], axis=0
            )
            for ci in range(2)
            for cj in range(2)
        ],
        axis=1,
    )
    sums = dot(left, kernel_two[...])
    for i in range(2):
        for j in range(2):
            at = 32 * i + 16 * j
            for h in range(2):
                keep = (pooled_three[i, j] & (15 << (4 * h))) != 0
                for t in range(2):
                    value = sums[at + 8 * h : at + 8 * h + 8, 128 * t : 128 * t + 128]
                    field_three[i, j, 2 * h + t] = jnp.where(keep, jnp.maximum(value, 0.0), 0.0)
    for to in range(2):
        for j in range(2):
            stage(2, to, j, [field_three[to, j, q] for q in range(4)])
    send(2)

    for i in range(2):
        fill_plane(2, cols_three, i + 1, lambda j, i=i: [field_three[i, j, q] for q in range(4)],
                   1, near, windows_three)
    loads[7].wait()
    early_three[...] = dot(
        columns(2, cols_three, range(2), range(3), WIDE_THREE, False),
        conv_three[...].reshape(27 * 256, 256),
    )
    turned = dot(regroup[...], done_two[...].reshape(256, 256))
    for t in range(2):
        wide[pl.ds(t, 256, stride=2), :] = turned[:, 128 * t : 128 * t + 128]
    out_two[...] = wide[...].reshape(BRICKS, 64, 128).astype(BF16)

    receive(2, cols_three, windows_three)

    for level in range(3):
        for to in range(2):
            @pl.when(sides[to][0])
            def _():
                transfer(level, to).wait_send()


def last_level(one, two, cols_three, pooled_three, early_three, conv_three,
               out_one, out_two, out_three, wide, sems):
    copies = [
        pltpu.make_async_copy(one, out_one, sems.at[0]),
        pltpu.make_async_copy(two, out_two, sems.at[1]),
    ]
    for copy in copies:
        copy.start()
    for i, sums in halo_sums(
        2, cols_three, WIDE_THREE, lambda a, depth: conv_three[9 * a : 9 * a + 9].reshape(depth, 256)
    ):
        sums = early_three[32 * i : 32 * i + 32] + sums
        for j in range(2):
            at = 16 * j
            for h in range(2):
                keep = (pooled_three[i, j] & (15 << (4 * h))) != 0
                for t in range(2):
                    value = sums[at + 8 * h : at + 8 * h + 8, 128 * t : 128 * t + 128]
                    wide[t, pl.ds(4 * i + 2 * j + h, 8, stride=8), :] = jnp.where(
                        keep, jnp.maximum(value, 0.0), 0.0
                    )
    for t in range(2):
        out_three[:, :, 128 * t : 128 * t + 128] = wide[t].reshape(BRICKS, 8, 128).astype(BF16)
    for copy in copies:
        copy.wait()


def on_device(features, neighbours, occupancy, conv_one, first_reduce_kernel,
              conv_two, second_reduce_kernel, conv_three):
    vm = pl.BlockSpec(memory_space=pltpu.VMEM)
    hbm = pl.BlockSpec(memory_space=pltpu.HBM)
    kernel_two = second_reduce_kernel.reshape(1024, 256)
    features, first_kernel = jnp.swapaxes(features, 1, 2), first_reduce_kernel.reshape(512, 128)
    scratch = [
        (neighbours.shape, I32), (features.shape, BF16), (occupancy.shape, I32),
        (conv_one.shape, BF16), (first_kernel.shape, BF16), (conv_two.shape, BF16), (kernel_two.shape, BF16),
        ((2048, 128), F32), ((4, 4, 4, BRICKS, 128), F32), ((2, 2, 4, BRICKS, 128), F32),
        ((10, 10, 16, 384), BF16), ((6, 6, 16, 512), BF16),
        ((8, 8, 16, 256), BF16), ((4, 4, 16, 256), BF16),
        ((9 * 384, 256), BF16), ((2, 128, 256), F32), ((2, 128, 128), F32),
        ((27, BRICKS, 128), I32), ((16, BRICKS, 128), I32), ((16, BRICKS, 128), I32),
        ((4, 4, BRICKS, 128), I32), ((512, 128), F32),
        ((128, 256), BF16), ((256, 256), BF16), ((256, 256), BF16),
        ((3, 2, 8, 16, 256), BF16), ((3, 2, 8, 16, 256), BF16),
    ]
    shapes = [
        jax.ShapeDtypeStruct((BRICKS, 64, 512), BF16),
        jax.ShapeDtypeStruct((BRICKS, 64, 128), BF16),
    ]
    first, second, cols, pooled, early, weights = pl.pallas_call(
        fused,
        out_shape=shapes
        + [
            jax.ShapeDtypeStruct((4, 4, 16, 768), BF16),
            jax.ShapeDtypeStruct((2, 2, BRICKS, 128), I32),
            jax.ShapeDtypeStruct((64, 256), F32),
            jax.ShapeDtypeStruct(conv_three.shape, BF16),
        ],
        in_specs=[hbm] * 8,
        out_specs=[vm] * 6,
        scratch_shapes=[pltpu.VMEM(shape, dtype) for shape, dtype in scratch]
        + [pltpu.SemaphoreType.DMA((8,)), pltpu.SemaphoreType.DMA((3, 2)),
           pltpu.SemaphoreType.DMA((3, 2))],
        compiler_params=pltpu.CompilerParams(
            collective_id=0, has_side_effects=True, vmem_limit_bytes=36 << 20
        ),
    )(*(
        pltpu.with_memory_space_constraint(x, pltpu.HBM)
        for x in (neighbours, features, occupancy, conv_one, first_kernel, conv_two, kernel_two, conv_three)
    ))
    first, second, third = pl.pallas_call(
        last_level,
        out_shape=shapes + [jax.ShapeDtypeStruct((BRICKS, 8, 256), BF16)],
        in_specs=[vm] * 6,
        out_specs=[hbm, hbm, vm],
        scratch_shapes=[pltpu.VMEM((2, 64, 128), F32), pltpu.SemaphoreType.DMA((2,))],
        compiler_params=pltpu.CompilerParams(vmem_limit_bytes=16 << 20),
    )(first, second, cols, pooled, early, weights)
    return jnp.swapaxes(first, 1, 2), second, third


def solution(mesh):
    split = P(("tiles", "morton"), None, None)
    flat = P(("tiles", "morton"), None)
    return jax.shard_map(
        on_device,
        mesh=mesh,
        in_specs=(split, flat, flat, P(), P(), P(), P(), P()),
        out_specs=(split, split, split),
        check_vma=False,
    )
```

```python
import jax
import jax.numpy as jnp
from jax import lax
from jax.experimental import pallas as pl
from jax.experimental.pallas import tpu as pltpu
from jax.sharding import PartitionSpec as P

BRICKS = 8
F32 = jnp.float32
BF16 = jnp.bfloat16
I32 = jnp.int32


def iota(shape, dim):
    return lax.broadcasted_iota(I32, shape, dim)


def pack(lower, upper):
    return jnp.concatenate([lower, upper], axis=0).astype(BF16)


def halves(tile):
    wide = tile.astype(F32)
    return wide[0:8], wide[8:16]


def windows_one(own, before, after):
    low_lanes = iota((BRICKS, 128), 1) < 64
    return (
        (own[0], own[2]),
        (own[1], own[3]),
        (jnp.where(low_lanes, own[2], before(3)), jnp.where(low_lanes, after(0), own[1])),
    )


def windows_two(own, before, after):
    return ((before(3), own[1]), (own[0], own[2]), (own[1], own[3]), (own[2], after(0)))


def windows_three(own, before, after):
    return (
        (before(2), own[0]), (before(3), own[1]),
        (own[0], own[2]), (own[1], own[3]),
        (own[2], after(0)), (own[3], after(1)),
    )


def fill(put, tiles, dx, dy, near, windows):
    first = 9 * dx + 3 * dy

    def moved(q, tap):
        number = near[tap]
        picked = jnp.take_along_axis(tiles[q], number & (BRICKS - 1), axis=0, mode="promise_in_bounds")
        return jnp.where(number >= 0, picked, 0.0)

    own = tiles if first == 12 else [moved(q, first + 1) for q in range(4)]
    for at, (lower, upper) in enumerate(
        windows(own, lambda q: moved(q, first), lambda q: moved(q, first + 2))
    ):
        put(at, pack(lower, upper))


def fill_plane(side, cols, to, source, dx, near, windows):
    for j in range(side):
        tiles = source(j)
        places = [(1, j + 1)] + [(0, 0)] * (j == side - 1) + [(2, side + 1)] * (j == 0)
        for dy, column in places:
            def put(at, value, column=column):
                cols[to, column, :, 128 * at : 128 * at + 128] = value
            fill(put, tiles, dx, dy, near, windows)


def columns(side, cols, planes, rows_of_taps, lanes, with_halo):
    def block(plane, c):
        if not with_halo and plane in (0, side + 1):
            return jnp.zeros((side * 16, lanes[0].stop - lanes[0].start), BF16)
        return [cols[plane, c : c + side, :, at].reshape(side * 16, at.stop - at.start) for at in lanes]

    def rows(a, c):
        blocks = [block(plane + a, c) for plane in planes]
        return jnp.concatenate(
            [part if not isinstance(part, list) else part[t] for t in range(len(lanes)) for part in blocks],
            axis=0,
        )

    return jnp.concatenate([rows(a, c) for a in rows_of_taps for c in range(3)], axis=1)


def build_band_one(source, band):
    @pl.loop(0, 9)
    def _(pair):
        minus, same, plus = (source[3 * pair + e] for e in range(3))
        zero = jnp.zeros_like(same)
        blank = jnp.zeros((64, 128), BF16)
        low = jnp.concatenate([same, minus], axis=1)
        high = jnp.concatenate([plus, same], axis=1)
        before = jnp.concatenate([minus, zero], axis=1)
        after = jnp.concatenate([zero, plus], axis=1)
        rows = ((low, blank), (high, before), (after, low), (blank, high), (blank, after), (before, blank))
        for at, (left, right) in enumerate(rows):
            to = pl.ds(pl.multiple_of(384 * pair + 64 * at, 64), 64)
            band[to, 0:128] = left
            band[to, 128:256] = right


WIDE_ONE = (slice(0, 384),)
WIDE_TWO = (slice(0, 384), slice(128, 512))
WIDE_THREE = (slice(0, 768),)


def dot(left, right):
    return jnp.dot(left, right, preferred_element_type=F32)


def halo_sums(side, cols, lanes, weights):
    for plane, a in ((0, 0), (side - 1, 2)):
        left = columns(side, cols, (plane,), (a,), lanes, True)
        depth = left.shape[1]
        yield plane, dot(left, weights(a, depth))


def fused(nb_hbm, feat_hbm, occ_hbm, conv_one_hbm, kernel_one_hbm,
          conv_two_hbm, kernel_two_hbm, conv_three_hbm,
          out_one, out_two, cols_three, pooled_three, early_three, conv_three,
          nb, feat, occ, conv_one, kernel_one, conv_two, kernel_two,
          field_one, field_two, field_three, cols_one, cols_two, done_one, done_two,
          band_one, early_one, early_two, near, words, tests, pooled_two, wide,
          choose, spread, regroup, outgoing, incoming, load_sems, send_sems, recv_sems):
    me = lax.axis_index("morton")
    count = lax.axis_size("morton")
    has_low, has_high = me > 0, me < count - 1
    sides = ((has_low, me - 1), (has_high, me + 1))
    extents = (8, 4, 2)

    loads = [
        pltpu.make_async_copy(source, target, load_sems.at[at])
        for at, (source, target) in enumerate(
            (
                (nb_hbm, nb), (occ_hbm, occ), (feat_hbm, feat), (conv_one_hbm, conv_one),
                (kernel_one_hbm, kernel_one), (conv_two_hbm, conv_two),
                (kernel_two_hbm, kernel_two), (conv_three_hbm, conv_three),
            )
        )
    ]
    for load in loads:
        load.start()

    barrier = pltpu.get_barrier_semaphore()
    for there, device in sides:
        @pl.when(there)
        def _():
            pl.semaphore_signal(barrier, inc=1, device_id={"morton": device},
                                device_id_type=pl.DeviceIdType.MESH)

    def transfer(level, to):
        return pltpu.make_async_remote_copy(
            src_ref=outgoing.at[level, to, 0 : extents[level]],
            dst_ref=incoming.at[level, 1 - to, 0 : extents[level]],
            send_sem=send_sems.at[level, to],
            recv_sem=recv_sems.at[level, 1 - to],
            device_id={"morton": sides[to][1]},
            device_id_type=pl.DeviceIdType.MESH,
        )

    def send(level):
        for to in range(2):
            @pl.when(sides[to][0])
            def _():
                transfer(level, to).start()

    def receive(level, cols, windows):
        side = extents[level]
        for source in range(2):
            @pl.when(sides[source][0])
            def _():
                transfer(level, 1 - source).wait_recv()

        for source in range(2):
            def arrived(j, source=source):
                pieces = [halves(incoming[level, source, j, :, 128 * t : 128 * t + 128]) for t in range(2)]
                return [pieces[q % 2][q // 2] for q in range(4)]

            fill_plane(side, cols, (0, side + 1)[source], arrived, 2 * source, near, windows)

    def stage(level, to, j, tiles):
        for t in range(2):
            outgoing[level, to, j, :, 128 * t : 128 * t + 128] = pack(tiles[t], tiles[2 + t])

    for source in range(2):
        @pl.when(jnp.logical_not(sides[source][0]))
        def _():
            for level in range(3):
                incoming[level, source] = jnp.zeros(incoming.shape[2:], BF16)

    row, lane = iota((256, 256), 0), iota((256, 256), 1)
    spread[...] = (lane == 2 * (row % 128) + row // 128).astype(F32).astype(BF16)
    regroup[...] = ((lane // 8 == row % 32) & (lane % 8 == row // 32)).astype(F32).astype(BF16)
    choose[...] = (iota((128, 256), 1) // 2 == iota((128, 256), 0)).astype(F32).astype(BF16)
    upper = (iota((BRICKS, 128), 1) >= 64).astype(I32)
    for at in range(16):
        tests[at] = jnp.left_shift(jnp.ones((BRICKS, 128), I32), 2 * at + upper)

    loads[0].wait()
    loads[1].wait()
    for tap in range(27):
        near[tap] = jnp.broadcast_to(nb[:, tap : tap + 1], (BRICKS, 128))
    for word in range(16):
        words[word] = jnp.broadcast_to(occ[:, word : word + 1], (BRICKS, 128))
    for i in range(4):
        for part in range(2):
            word = words[4 * i + part] | words[4 * i + 2 + part]
            for far in range(2):
                pooled_two[i, 2 * part + far] = (word >> (16 * far)) | (word >> (16 * far + 8))
    for i in range(2):
        for j in range(2):
            pooled_three[i, j] = (
                pooled_two[2 * i, 2 * j] | pooled_two[2 * i, 2 * j + 1]
                | pooled_two[2 * i + 1, 2 * j] | pooled_two[2 * i + 1, 2 * j + 1]
            )

    def keep_one(i, j, q, value):
        bit = words[2 * i + j // 4] & tests[4 * (j % 4) + q]
        return jnp.where(bit != 0, value, 0.0)

    loads[2].wait()
    odd = iota((64, 256), 1) % 2 == 1
    for half in range(2):
        lanes = slice(256 * half, 256 * half + 256)
        for b in range(0, BRICKS, 2):
            rows = []
            for brick in (b, b + 1):
                value = feat[brick, :, lanes]
                zero = jnp.zeros_like(value)
                rows += [jnp.where(odd, zero, value), jnp.where(odd, value, zero)]
            both = lax.dot_general(
                choose[...], jnp.concatenate(rows, axis=0), (((1,), (1,)), ((), ())),
                preferred_element_type=F32,
            )
            for step in range(2):
                field_one[pl.ds(1024 * half + b + step, 128, stride=8), :] = (
                    both[:, 128 * step : 128 * step + 128]
                )

    def tile_at(i, j, q):
        return pl.ds(pl.multiple_of(256 * i + 32 * j + 8 * q, 8), 8)

    def own_one(i):
        def source(j):
            return [keep_one(i, j, q, field_one[tile_at(i, j, q), :]) for q in range(4)]
        return source

    for to, i in enumerate((0, 7)):
        def edge(j, to=to, i=i):
            tiles = own_one(i)(j)
            stage(0, to, j, tiles)
            return tiles
        fill_plane(8, cols_one, i + 1, edge, 1, near, windows_one)

    pl.semaphore_wait(barrier, jnp.minimum(me, 1) + jnp.minimum(count - 1 - me, 1))
    send(0)
    loads[3].wait()
    loads[4].wait()
    build_band_one(conv_one, band_one)

    @pl.loop(1, 7)
    def _(i):
        fill_plane(8, cols_one, i + 1, own_one(i), 1, near, windows_one)

    def finish_one(i, sums):
        for j in range(8):
            for t in range(2):
                lanes = slice(128 * t, 128 * t + 128)
                tiles = []
                for h in range(2):
                    q = 2 * h + t
                    at = 16 * j + 8 * h
                    value = keep_one(i, j, q, jnp.maximum(sums[at : at + 8, lanes], 0.0))
                    field_one[tile_at(i, j, q), :] = value
                    tiles.append(value)
                done_one[i, j, :, lanes] = pack(*tiles)

    def reduce_one(pooled):
        left = jnp.concatenate(
            [
                jnp.concatenate(
                    [
                        done_one[2 * i + ci, 2 * j + cj, :, 128 * t : 128 * t + 128]
                        for t in range(2)
                        for i in pooled
                        for j in range(4)
                    ],
                    axis=0,
                )
                for ci in range(2)
                for cj in range(2)
            ],
            axis=1,
        )
        sums = dot(left, kernel_one[...])
        for p, i in enumerate(pooled):
            for j in range(4):
                for t in range(2):
                    for h in range(2):
                        at = 128 * t + 64 * p + 16 * j + 8 * h
                        q = 2 * h + t
                        keep = (pooled_two[i, j] & (3 << (2 * q))) != 0
                        field_two[i, j, q] = jnp.where(keep, jnp.maximum(sums[at : at + 8], 0.0), 0.0)

    def own_two(i):
        return lambda j: [field_two[i, j, q] for q in range(4)]

    sums = dot(columns(8, cols_one, range(8), range(3), WIDE_ONE, False), band_one[...])
    for i in range(8):
        part = sums[128 * i : 128 * i + 128]
        if i in (0, 7):
            early_one[i // 7] = part
        else:
            finish_one(i, part)
    reduce_one((1, 2))
    for load in loads[5:]:
        load.wait()
    receive(0, cols_one, windows_one)
    for i, sums in halo_sums(8, cols_one, WIDE_ONE, lambda a, depth: band_one[a * depth : (a + 1) * depth]):
        finish_one(i, early_one[i // 7] + sums)
    reduce_one((0, 3))
    for to, i in enumerate((0, 3)):
        for j in range(4):
            stage(1, to, j, own_two(i)(j))
    send(1)

    def finish_two(i, sums):
        for j in range(4):
            for t in range(2):
                tiles = []
                for h in range(2):
                    q = 2 * h + t
                    at = 64 * t + 16 * j + 8 * h
                    keep = (pooled_two[i, j] & (3 << (2 * q))) != 0
                    tiles.append(jnp.where(keep, jnp.maximum(sums[at : at + 8], 0.0), 0.0))
                done_two[i, j, :, 128 * t : 128 * t + 128] = pack(*tiles)

    for i in range(4):
        fill_plane(4, cols_two, i + 1, own_two(i), 1, near, windows_two)
    sums = dot(
        columns(4, cols_two, range(4), range(3), WIDE_TWO, False),
        conv_two[...].reshape(27 * 128, 128),
    )
    for i in range(4):
        part = jnp.concatenate([sums[256 * t + 64 * i : 256 * t + 64 * i + 64] for t in range(2)], axis=0)
        if i in (0, 3):
            early_two[i // 3] = part
        else:
            finish_two(i, part)

    for half in range(2):
        left = []
        for b in range(BRICKS):
            turned = field_one[pl.ds(1024 * half + b, 128, stride=8), :].astype(BF16).T
            left.append(jnp.concatenate([turned[0:64], turned[64:128]], axis=1))
        sums = dot(jnp.concatenate(left, axis=0), spread[...])
        for b in range(BRICKS):
            out_one[b, :, 256 * half : 256 * half + 256] = sums[64 * b : 64 * b + 64].astype(BF16)

    receive(1, cols_two, windows_two)
    for i, sums in halo_sums(
        4, cols_two, WIDE_TWO, lambda a, depth: conv_two[9 * a : 9 * a + 9].reshape(depth, 128)
    ):
        finish_two(i, early_two[i // 3] + sums)
    left = jnp.concatenate(
        [
            jnp.concatenate(
                [done_two[2 * i + ci, 2 * j + cj] for i in range(2) for j in range(2)], axis=0
            )
            for ci in range(2)
            for cj in range(2)
        ],
        axis=1,
    )
    sums = dot(left, kernel_two[...])
    for i in range(2):
        for j in range(2):
            at = 32 * i + 16 * j
            for h in range(2):
                keep = (pooled_three[i, j] & (15 << (4 * h))) != 0
                for t in range(2):
                    value = sums[at + 8 * h : at + 8 * h + 8, 128 * t : 128 * t + 128]
                    field_three[i, j, 2 * h + t] = jnp.where(keep, jnp.maximum(value, 0.0), 0.0)
    for to in range(2):
        for j in range(2):
            stage(2, to, j, [field_three[to, j, q] for q in range(4)])
    send(2)

    for i in range(2):
        fill_plane(2, cols_three, i + 1, lambda j, i=i: [field_three[i, j, q] for q in range(4)],
                   1, near, windows_three)
    early_three[...] = dot(
        columns(2, cols_three, range(2), range(3), WIDE_THREE, False),
        conv_three[...].reshape(27 * 256, 256),
    )
    turned = dot(regroup[...], done_two[...].reshape(256, 256))
    for t in range(2):
        wide[pl.ds(t, 256, stride=2), :] = turned[:, 128 * t : 128 * t + 128]
    out_two[...] = wide[...].reshape(BRICKS, 64, 128).astype(BF16)

    receive(2, cols_three, windows_three)

    for level in range(3):
        for to in range(2):
            @pl.when(sides[to][0])
            def _():
                transfer(level, to).wait_send()


def last_level(one, two, cols_three, pooled_three, early_three, conv_three,
               out_one, out_two, out_three, wide, sems):
    def copies(half):
        bricks = pl.ds(BRICKS // 2 * half, BRICKS // 2)
        return [
            pltpu.make_async_copy(source.at[bricks], target.at[bricks], sems.at[at, half])
            for at, (source, target) in enumerate(((one, out_one), (two, out_two)))
        ]

    @pl.loop(0, 2)
    def _(half):
        for copy in copies(half):
            copy.start()

    for i, sums in halo_sums(
        2, cols_three, WIDE_THREE, lambda a, depth: conv_three[9 * a : 9 * a + 9].reshape(depth, 256)
    ):
        sums = early_three[32 * i : 32 * i + 32] + sums
        for j in range(2):
            at = 16 * j
            for h in range(2):
                keep = (pooled_three[i, j] & (15 << (4 * h))) != 0
                for t in range(2):
                    value = sums[at + 8 * h : at + 8 * h + 8, 128 * t : 128 * t + 128]
                    wide[t, pl.ds(4 * i + 2 * j + h, 8, stride=8), :] = jnp.where(
                        keep, jnp.maximum(value, 0.0), 0.0
                    )
    for t in range(2):
        out_three[:, :, 128 * t : 128 * t + 128] = wide[t].reshape(BRICKS, 8, 128).astype(BF16)
    for half in range(2):
        for copy in copies(half):
            copy.wait()


def on_device(features, neighbours, occupancy, conv_one, first_reduce_kernel,
              conv_two, second_reduce_kernel, conv_three):
    vm = pl.BlockSpec(memory_space=pltpu.VMEM)
    hbm = pl.BlockSpec(memory_space=pltpu.HBM)
    kernel_two = second_reduce_kernel.reshape(1024, 256)
    features, first_kernel = jnp.swapaxes(features, 1, 2), first_reduce_kernel.reshape(512, 128)
    scratch = [
        (neighbours.shape, I32), (features.shape, BF16), (occupancy.shape, I32),
        (conv_one.shape, BF16), (first_kernel.shape, BF16), (conv_two.shape, BF16), (kernel_two.shape, BF16),
        ((2048, 128), F32), ((4, 4, 4, BRICKS, 128), F32), ((2, 2, 4, BRICKS, 128), F32),
        ((10, 10, 16, 384), BF16), ((6, 6, 16, 512), BF16),
        ((8, 8, 16, 256), BF16), ((4, 4, 16, 256), BF16),
        ((9 * 384, 256), BF16), ((2, 128, 256), F32), ((2, 128, 128), F32),
        ((27, BRICKS, 128), I32), ((16, BRICKS, 128), I32), ((16, BRICKS, 128), I32),
        ((4, 4, BRICKS, 128), I32), ((512, 128), F32),
        ((128, 256), BF16), ((256, 256), BF16), ((256, 256), BF16),
        ((3, 2, 8, 16, 256), BF16), ((3, 2, 8, 16, 256), BF16),
    ]
    shapes = [
        jax.ShapeDtypeStruct((BRICKS, 64, 512), BF16),
        jax.ShapeDtypeStruct((BRICKS, 64, 128), BF16),
    ]
    first, second, cols, pooled, early, weights = pl.pallas_call(
        fused,
        out_shape=shapes
        + [
            jax.ShapeDtypeStruct((4, 4, 16, 768), BF16),
            jax.ShapeDtypeStruct((2, 2, BRICKS, 128), I32),
            jax.ShapeDtypeStruct((64, 256), F32),
            jax.ShapeDtypeStruct(conv_three.shape, BF16),
        ],
        in_specs=[hbm] * 8,
        out_specs=[vm] * 6,
        scratch_shapes=[pltpu.VMEM(shape, dtype) for shape, dtype in scratch]
        + [pltpu.SemaphoreType.DMA((8,)), pltpu.SemaphoreType.DMA((3, 2)),
           pltpu.SemaphoreType.DMA((3, 2))],
        compiler_params=pltpu.CompilerParams(
            collective_id=0, has_side_effects=True,
            vmem_limit_bytes=36 << 20
        ),
    )(*(
        pltpu.with_memory_space_constraint(x, pltpu.HBM)
        for x in (neighbours, features, occupancy, conv_one, first_kernel, conv_two, kernel_two, conv_three)
    ))
    first, second, third = pl.pallas_call(
        last_level,
        out_shape=shapes + [jax.ShapeDtypeStruct((BRICKS, 8, 256), BF16)],
        in_specs=[vm] * 6,
        out_specs=[hbm, hbm, vm],
        scratch_shapes=[pltpu.VMEM((2, 64, 128), F32), pltpu.SemaphoreType.DMA((2, 2))],
        compiler_params=pltpu.CompilerParams(vmem_limit_bytes=16 << 20),
    )(first, second, cols, pooled, early, weights)
    return jnp.swapaxes(first, 1, 2), second, third


def solution(mesh):
    split = P(("tiles", "morton"), None, None)
    flat = P(("tiles", "morton"), None)
    return jax.shard_map(
        on_device,
        mesh=mesh,
        in_specs=(split, flat, flat, P(), P(), P(), P(), P()),
        out_specs=(split, split, split),
        check_vma=False,
    )
```

```python
import jax
import jax.numpy as jnp
from jax import lax
from jax.experimental import pallas as pl
from jax.experimental.pallas import tpu as pltpu
from jax.sharding import PartitionSpec as P

BRICKS = 8
F32 = jnp.float32
BF16 = jnp.bfloat16
I32 = jnp.int32


def iota(shape, dim):
    return lax.broadcasted_iota(I32, shape, dim)


def pack(lower, upper):
    return jnp.concatenate([lower, upper], axis=0).astype(BF16)


def halves(tile):
    wide = tile.astype(F32)
    return wide[0:8], wide[8:16]


def windows_one(own, before, after):
    low_lanes = iota((BRICKS, 128), 1) < 64
    return (
        (own[0], own[2]),
        (own[1], own[3]),
        (jnp.where(low_lanes, own[2], before(3)), jnp.where(low_lanes, after(0), own[1])),
    )


def windows_two(own, before, after):
    return ((before(3), own[1]), (own[0], own[2]), (own[1], own[3]), (own[2], after(0)))


def windows_three(own, before, after):
    return (
        (before(2), own[0]), (before(3), own[1]),
        (own[0], own[2]), (own[1], own[3]),
        (own[2], after(0)), (own[3], after(1)),
    )


def fill(put, tiles, dx, dy, near, windows):
    first = 9 * dx + 3 * dy

    def moved(q, tap):
        number = near[tap]
        picked = jnp.take_along_axis(tiles[q], number & (BRICKS - 1), axis=0, mode="promise_in_bounds")
        return jnp.where(number >= 0, picked, 0.0)

    own = tiles if first == 12 else [moved(q, first + 1) for q in range(4)]
    for at, (lower, upper) in enumerate(
        windows(own, lambda q: moved(q, first), lambda q: moved(q, first + 2))
    ):
        put(at, pack(lower, upper))


def fill_plane(side, cols, to, source, dx, near, windows):
    for j in range(side):
        tiles = source(j)
        places = [(1, j + 1)] + [(0, 0)] * (j == side - 1) + [(2, side + 1)] * (j == 0)
        for dy, column in places:
            def put(at, value, column=column):
                cols[to, column, :, 128 * at : 128 * at + 128] = value
            fill(put, tiles, dx, dy, near, windows)


def columns(side, cols, planes, rows_of_taps, lanes, with_halo):
    def block(plane, c):
        if not with_halo and plane in (0, side + 1):
            return jnp.zeros((side * 16, lanes[0].stop - lanes[0].start), BF16)
        return [cols[plane, c : c + side, :, at].reshape(side * 16, at.stop - at.start) for at in lanes]

    def rows(a, c):
        blocks = [block(plane + a, c) for plane in planes]
        return jnp.concatenate(
            [part if not isinstance(part, list) else part[t] for t in range(len(lanes)) for part in blocks],
            axis=0,
        )

    return jnp.concatenate([rows(a, c) for a in rows_of_taps for c in range(3)], axis=1)


def build_band_one(source, band):
    for pair in range(9):
        minus, same, plus = (source[3 * pair + e] for e in range(3))
        zero = jnp.zeros_like(same)
        blank = jnp.zeros((64, 128), BF16)
        low = jnp.concatenate([same, minus], axis=1)
        high = jnp.concatenate([plus, same], axis=1)
        before = jnp.concatenate([minus, zero], axis=1)
        after = jnp.concatenate([zero, plus], axis=1)
        rows = ((low, blank), (high, before), (after, low), (blank, high), (blank, after), (before, blank))
        for at, (left, right) in enumerate(rows):
            to = slice(384 * pair + 64 * at, 384 * pair + 64 * at + 64)
            band[to, 0:128] = left
            band[to, 128:256] = right


WIDE_ONE = (slice(0, 384),)
WIDE_TWO = (slice(0, 384), slice(128, 512))
WIDE_THREE = (slice(0, 768),)


def dot(left, right):
    return jnp.dot(left, right, preferred_element_type=F32)


def halo_sums(side, cols, lanes, weights):
    for plane, a in ((0, 0), (side - 1, 2)):
        left = columns(side, cols, (plane,), (a,), lanes, True)
        depth = left.shape[1]
        yield plane, dot(left, weights(a, depth))


def fused(nb_hbm, feat_hbm, occ_hbm, conv_one_hbm, kernel_one_hbm,
          conv_two_hbm, kernel_two_hbm, conv_three_hbm,
          out_one, out_two, cols_three, pooled_three, early_three, conv_three,
          nb, feat, occ, conv_one, kernel_one, conv_two, kernel_two,
          field_one, field_two, field_three, cols_one, cols_two, done_one, done_two,
          band_one, early_one, early_two, near, words, tests, pooled_two, wide,
          choose, spread, regroup, outgoing, incoming, load_sems, send_sems, recv_sems):
    me = lax.axis_index("morton")
    count = lax.axis_size("morton")
    has_low, has_high = me > 0, me < count - 1
    sides = ((has_low, me - 1), (has_high, me + 1))
    extents = (8, 4, 2)

    loads = [
        pltpu.make_async_copy(source, target, load_sems.at[at])
        for at, (source, target) in enumerate(
            (
                (nb_hbm, nb), (occ_hbm, occ), (conv_one_hbm, conv_one), (feat_hbm, feat),
                (kernel_one_hbm, kernel_one), (conv_two_hbm, conv_two),
                (kernel_two_hbm, kernel_two), (conv_three_hbm, conv_three),
            )
        )
    ]
    for load in loads:
        load.start()

    barrier = pltpu.get_barrier_semaphore()
    for there, device in sides:
        @pl.when(there)
        def _():
            pl.semaphore_signal(barrier, inc=1, device_id={"morton": device},
                                device_id_type=pl.DeviceIdType.MESH)

    def transfer(level, to):
        return pltpu.make_async_remote_copy(
            src_ref=outgoing.at[level, to, 0 : extents[level]],
            dst_ref=incoming.at[level, 1 - to, 0 : extents[level]],
            send_sem=send_sems.at[level, to],
            recv_sem=recv_sems.at[level, 1 - to],
            device_id={"morton": sides[to][1]},
            device_id_type=pl.DeviceIdType.MESH,
        )

    def send(level):
        for to in range(2):
            @pl.when(sides[to][0])
            def _():
                transfer(level, to).start()

    def receive(level, cols, windows):
        side = extents[level]
        for source in range(2):
            @pl.when(sides[source][0])
            def _():
                transfer(level, 1 - source).wait_recv()

        for source in range(2):
            def arrived(j, source=source):
                pieces = [halves(incoming[level, source, j, :, 128 * t : 128 * t + 128]) for t in range(2)]
                return [pieces[q % 2][q // 2] for q in range(4)]

            fill_plane(side, cols, (0, side + 1)[source], arrived, 2 * source, near, windows)

    def stage(level, to, j, tiles):
        for t in range(2):
            outgoing[level, to, j, :, 128 * t : 128 * t + 128] = pack(tiles[t], tiles[2 + t])

    for source in range(2):
        @pl.when(jnp.logical_not(sides[source][0]))
        def _():
            for level in range(3):
                incoming[level, source] = jnp.zeros(incoming.shape[2:], BF16)

    row, lane = iota((256, 256), 0), iota((256, 256), 1)
    spread[...] = (lane == 2 * (row % 128) + row // 128).astype(F32).astype(BF16)
    regroup[...] = ((lane // 8 == row % 32) & (lane % 8 == row // 32)).astype(F32).astype(BF16)
    choose[...] = (iota((128, 256), 1) // 2 == iota((128, 256), 0)).astype(F32).astype(BF16)
    upper = (iota((BRICKS, 128), 1) >= 64).astype(I32)
    for at in range(16):
        tests[at] = jnp.left_shift(jnp.ones((BRICKS, 128), I32), 2 * at + upper)

    loads[0].wait()
    loads[1].wait()
    for tap in range(27):
        near[tap] = jnp.broadcast_to(nb[:, tap : tap + 1], (BRICKS, 128))
    for word in range(16):
        words[word] = jnp.broadcast_to(occ[:, word : word + 1], (BRICKS, 128))
    for i in range(4):
        for part in range(2):
            word = words[4 * i + part] | words[4 * i + 2 + part]
            for far in range(2):
                pooled_two[i, 2 * part + far] = (word >> (16 * far)) | (word >> (16 * far + 8))
    for i in range(2):
        for j in range(2):
            pooled_three[i, j] = (
                pooled_two[2 * i, 2 * j] | pooled_two[2 * i, 2 * j + 1]
                | pooled_two[2 * i + 1, 2 * j] | pooled_two[2 * i + 1, 2 * j + 1]
            )

    def keep_one(i, j, q, value):
        bit = words[2 * i + j // 4] & tests[4 * (j % 4) + q]
        return jnp.where(bit != 0, value, 0.0)

    loads[2].wait()
    build_band_one(conv_one, band_one)
    loads[3].wait()
    odd = iota((64, 256), 1) % 2 == 1
    for half in range(2):
        lanes = slice(256 * half, 256 * half + 256)
        for b in range(0, BRICKS, 2):
            rows = []
            for brick in (b, b + 1):
                value = feat[brick, :, lanes]
                zero = jnp.zeros_like(value)
                rows += [jnp.where(odd, zero, value), jnp.where(odd, value, zero)]
            both = lax.dot_general(
                choose[...], jnp.concatenate(rows, axis=0), (((1,), (1,)), ((), ())),
                preferred_element_type=F32,
            )
            for step in range(2):
                field_one[pl.ds(1024 * half + b + step, 128, stride=8), :] = (
                    both[:, 128 * step : 128 * step + 128]
                )

    def tile_at(i, j, q):
        return pl.ds(pl.multiple_of(256 * i + 32 * j + 8 * q, 8), 8)

    def own_one(i):
        def source(j):
            return [keep_one(i, j, q, field_one[tile_at(i, j, q), :]) for q in range(4)]
        return source

    for to, i in enumerate((0, 7)):
        def edge(j, to=to, i=i):
            tiles = own_one(i)(j)
            stage(0, to, j, tiles)
            return tiles
        fill_plane(8, cols_one, i + 1, edge, 1, near, windows_one)

    pl.semaphore_wait(barrier, jnp.minimum(me, 1) + jnp.minimum(count - 1 - me, 1))
    send(0)
    loads[4].wait()

    @pl.loop(1, 7)
    def _(i):
        fill_plane(8, cols_one, i + 1, own_one(i), 1, near, windows_one)

    def finish_one(i, sums):
        for j in range(8):
            for t in range(2):
                lanes = slice(128 * t, 128 * t + 128)
                tiles = []
                for h in range(2):
                    q = 2 * h + t
                    at = 16 * j + 8 * h
                    value = keep_one(i, j, q, jnp.maximum(sums[at : at + 8, lanes], 0.0))
                    field_one[tile_at(i, j, q), :] = value
                    tiles.append(value)
                done_one[i, j, :, lanes] = pack(*tiles)

    def reduce_one(pooled):
        left = jnp.concatenate(
            [
                jnp.concatenate(
                    [
                        done_one[2 * i + ci, 2 * j + cj, :, 128 * t : 128 * t + 128]
                        for t in range(2)
                        for i in pooled
                        for j in range(4)
                    ],
                    axis=0,
                )
                for ci in range(2)
                for cj in range(2)
            ],
            axis=1,
        )
        sums = dot(left, kernel_one[...])
        for p, i in enumerate(pooled):
            for j in range(4):
                for t in range(2):
                    for h in range(2):
                        at = 128 * t + 64 * p + 16 * j + 8 * h
                        q = 2 * h + t
                        keep = (pooled_two[i, j] & (3 << (2 * q))) != 0
                        field_two[i, j, q] = jnp.where(keep, jnp.maximum(sums[at : at + 8], 0.0), 0.0)

    def own_two(i):
        return lambda j: [field_two[i, j, q] for q in range(4)]

    sums = dot(columns(8, cols_one, range(8), range(3), WIDE_ONE, False), band_one[...])
    for i in range(8):
        part = sums[128 * i : 128 * i + 128]
        if i in (0, 7):
            early_one[i // 7] = part
        else:
            finish_one(i, part)
    for load in loads[5:]:
        load.wait()
    receive(0, cols_one, windows_one)
    for i, sums in halo_sums(8, cols_one, WIDE_ONE, lambda a, depth: band_one[a * depth : (a + 1) * depth]):
        finish_one(i, early_one[i // 7] + sums)
    reduce_one((0, 3))
    for to, i in enumerate((0, 3)):
        for j in range(4):
            stage(1, to, j, own_two(i)(j))
    send(1)
    reduce_one((1, 2))

    def finish_two(i, sums):
        for j in range(4):
            for t in range(2):
                tiles = []
                for h in range(2):
                    q = 2 * h + t
                    at = 64 * t + 16 * j + 8 * h
                    keep = (pooled_two[i, j] & (3 << (2 * q))) != 0
                    tiles.append(jnp.where(keep, jnp.maximum(sums[at : at + 8], 0.0), 0.0))
                done_two[i, j, :, 128 * t : 128 * t + 128] = pack(*tiles)

    for i in range(4):
        fill_plane(4, cols_two, i + 1, own_two(i), 1, near, windows_two)
    sums = dot(
        columns(4, cols_two, range(4), range(3), WIDE_TWO, False),
        conv_two[...].reshape(27 * 128, 128),
    )
    for i in range(4):
        part = jnp.concatenate([sums[256 * t + 64 * i : 256 * t + 64 * i + 64] for t in range(2)], axis=0)
        if i in (0, 3):
            early_two[i // 3] = part
        else:
            finish_two(i, part)

    for half in range(2):
        left = []
        for b in range(BRICKS):
            turned = field_one[pl.ds(1024 * half + b, 128, stride=8), :].astype(BF16).T
            left.append(jnp.concatenate([turned[0:64], turned[64:128]], axis=1))
        sums = dot(jnp.concatenate(left, axis=0), spread[...])
        for b in range(BRICKS):
            out_one[b, :, 256 * half : 256 * half + 256] = sums[64 * b : 64 * b + 64].astype(BF16)

    receive(1, cols_two, windows_two)
    for i, sums in halo_sums(
        4, cols_two, WIDE_TWO, lambda a, depth: conv_two[9 * a : 9 * a + 9].reshape(depth, 128)
    ):
        finish_two(i, early_two[i // 3] + sums)
    left = jnp.concatenate(
        [
            jnp.concatenate(
                [done_two[2 * i + ci, 2 * j + cj] for i in range(2) for j in range(2)], axis=0
            )
            for ci in range(2)
            for cj in range(2)
        ],
        axis=1,
    )
    sums = dot(left, kernel_two[...])
    for i in range(2):
        for j in range(2):
            at = 32 * i + 16 * j
            for h in range(2):
                keep = (pooled_three[i, j] & (15 << (4 * h))) != 0
                for t in range(2):
                    value = sums[at + 8 * h : at + 8 * h + 8, 128 * t : 128 * t + 128]
                    field_three[i, j, 2 * h + t] = jnp.where(keep, jnp.maximum(value, 0.0), 0.0)
    for to in range(2):
        for j in range(2):
            stage(2, to, j, [field_three[to, j, q] for q in range(4)])
    send(2)

    for i in range(2):
        fill_plane(2, cols_three, i + 1, lambda j, i=i: [field_three[i, j, q] for q in range(4)],
                   1, near, windows_three)
    early_three[...] = dot(
        columns(2, cols_three, range(2), range(3), WIDE_THREE, False),
        conv_three[...].reshape(27 * 256, 256),
    )
    turned = dot(regroup[...], done_two[...].reshape(256, 256))
    for t in range(2):
        wide[pl.ds(t, 256, stride=2), :] = turned[:, 128 * t : 128 * t + 128]
    out_two[...] = wide[...].reshape(BRICKS, 64, 128).astype(BF16)

    receive(2, cols_three, windows_three)

    for level in range(3):
        for to in range(2):
            @pl.when(sides[to][0])
            def _():
                transfer(level, to).wait_send()


def last_level(one, two, cols_three, pooled_three, early_three, conv_three,
               out_one, out_two, out_three, wide, sems):
    def copies(half):
        bricks = pl.ds(BRICKS // 2 * half, BRICKS // 2)
        return [
            pltpu.make_async_copy(source.at[bricks], target.at[bricks], sems.at[at, half])
            for at, (source, target) in enumerate(((one, out_one), (two, out_two)))
        ]

    @pl.loop(0, 2)
    def _(half):
        for copy in copies(half):
            copy.start()

    for i, sums in halo_sums(
        2, cols_three, WIDE_THREE, lambda a, depth: conv_three[9 * a : 9 * a + 9].reshape(depth, 256)
    ):
        sums = early_three[32 * i : 32 * i + 32] + sums
        for j in range(2):
            at = 16 * j
            for h in range(2):
                keep = (pooled_three[i, j] & (15 << (4 * h))) != 0
                for t in range(2):
                    value = sums[at + 8 * h : at + 8 * h + 8, 128 * t : 128 * t + 128]
                    wide[t, pl.ds(4 * i + 2 * j + h, 8, stride=8), :] = jnp.where(
                        keep, jnp.maximum(value, 0.0), 0.0
                    )
    for t in range(2):
        out_three[:, :, 128 * t : 128 * t + 128] = wide[t].reshape(BRICKS, 8, 128).astype(BF16)
    for half in range(2):
        for copy in copies(half):
            copy.wait()


def on_device(features, neighbours, occupancy, conv_one, first_reduce_kernel,
              conv_two, second_reduce_kernel, conv_three):
    vm = pl.BlockSpec(memory_space=pltpu.VMEM)
    hbm = pl.BlockSpec(memory_space=pltpu.HBM)
    kernel_two = second_reduce_kernel.reshape(1024, 256)
    features, first_kernel = jnp.swapaxes(features, 1, 2), first_reduce_kernel.reshape(512, 128)
    scratch = [
        (neighbours.shape, I32), (features.shape, BF16), (occupancy.shape, I32),
        (conv_one.shape, BF16), (first_kernel.shape, BF16), (conv_two.shape, BF16), (kernel_two.shape, BF16),
        ((2048, 128), F32), ((4, 4, 4, BRICKS, 128), F32), ((2, 2, 4, BRICKS, 128), F32),
        ((10, 10, 16, 384), BF16), ((6, 6, 16, 512), BF16),
        ((8, 8, 16, 256), BF16), ((4, 4, 16, 256), BF16),
        ((9 * 384, 256), BF16), ((2, 128, 256), F32), ((2, 128, 128), F32),
        ((27, BRICKS, 128), I32), ((16, BRICKS, 128), I32), ((16, BRICKS, 128), I32),
        ((4, 4, BRICKS, 128), I32), ((512, 128), F32),
        ((128, 256), BF16), ((256, 256), BF16), ((256, 256), BF16),
        ((3, 2, 8, 16, 256), BF16), ((3, 2, 8, 16, 256), BF16),
    ]
    shapes = [
        jax.ShapeDtypeStruct((BRICKS, 64, 512), BF16),
        jax.ShapeDtypeStruct((BRICKS, 64, 128), BF16),
    ]
    first, second, cols, pooled, early, weights = pl.pallas_call(
        fused,
        out_shape=shapes
        + [
            jax.ShapeDtypeStruct((4, 4, 16, 768), BF16),
            jax.ShapeDtypeStruct((2, 2, BRICKS, 128), I32),
            jax.ShapeDtypeStruct((64, 256), F32),
            jax.ShapeDtypeStruct(conv_three.shape, BF16),
        ],
        in_specs=[hbm] * 8,
        out_specs=[vm] * 6,
        scratch_shapes=[pltpu.VMEM(shape, dtype) for shape, dtype in scratch]
        + [pltpu.SemaphoreType.DMA((8,)), pltpu.SemaphoreType.DMA((3, 2)),
           pltpu.SemaphoreType.DMA((3, 2))],
        compiler_params=pltpu.CompilerParams(
            collective_id=0, has_side_effects=True,
            vmem_limit_bytes=36 << 20
        ),
    )(*(
        pltpu.with_memory_space_constraint(x, pltpu.HBM)
        for x in (neighbours, features, occupancy, conv_one, first_kernel, conv_two, kernel_two, conv_three)
    ))
    first, second, third = pl.pallas_call(
        last_level,
        out_shape=shapes + [jax.ShapeDtypeStruct((BRICKS, 8, 256), BF16)],
        in_specs=[vm] * 6,
        out_specs=[hbm, hbm, vm],
        scratch_shapes=[pltpu.VMEM((2, 64, 128), F32), pltpu.SemaphoreType.DMA((2, 2))],
        compiler_params=pltpu.CompilerParams(vmem_limit_bytes=16 << 20),
    )(first, second, cols, pooled, early, weights)
    return jnp.swapaxes(first, 1, 2), second, third


def solution(mesh):
    split = P(("tiles", "morton"), None, None)
    flat = P(("tiles", "morton"), None)
    return jax.shard_map(
        on_device,
        mesh=mesh,
        in_specs=(split, flat, flat, P(), P(), P(), P(), P()),
        out_specs=(split, split, split),
        check_vma=False,
    )
```
